512 devices in a mesh: pts: 128 (over z, y, core), rhs: 4 (over x).
Axes of the slice: x: 4, y: 8, z: 8, core: 2. Of those that a mesh axis runs over, the one named last changes fastest.
Arguments:
- points: bfloat16 [3, 524288], P(None, 'pts'), may hold values from -4 to 4
- values: bfloat16 [64, 524288], P('rhs', 'pts'), may hold values from -6 to 6
- leaf_basis: bfloat16 [32, 524288], P(None, 'pts'), may hold values from -0.75 to 0.75
- local_transfer: bfloat16 [16128, 32, 32], P('pts'), may hold values from -0.75 to 0.75
- upper_transfer: bfloat16 [254, 32, 32], replicated, may hold values from -0.75 to 0.75
- local_coupling: bfloat16 [16128, 4, 32, 32], P('pts'), may hold values from -0.5 to 0.5
- upper_coupling: bfloat16 [254, 4, 32, 32], replicated, may hold values from -0.5 to 0.5
- near_list: int32 [8192, 8], P('pts'), may hold values from -1 to 8191, as said below
- local_partners: int32 [16128, 4], P('pts'), may hold values from -1 to 8191, as said below
- upper_partners: int32 [254, 4], replicated, may hold values from -1 to 127, as said below
Outputs:
- product: bfloat16 [64, 524288], P('rhs', 'pts')
The draws below stay inside these ranges and needn't reach their ends.
Inputs may be any that keep to these rules, and one draw needn't show every extreme that they name: `near_list`: entry 0 of row i is i itself; the other entries are -1 or distinct leaves at most 32 places from i. Some row has all 8 entries live, with offsets of both -32 and 32. `local_partners`: A row of level l (rows laid out as in the reference program, n = 64 / 2^l) holds -1 or distinct other clusters of level l, given by their index on that level, at most n places from its own cluster. On every level some row holds offsets of both -n and n; some row has 4 live entries. `upper_partners`: A row of level 6 + k holds -1 or distinct other clusters of that level, given by their index on that level.
All inputs are finite; a program needn't handle non-finite values.
Results may differ from the reference program's by a relative error of at most 0.013.
Values may be sent and summed in bfloat16 or wider, within the bound.
No kernel may reach another device: no remote copies, remote signals or barrier semaphores. Data moves between devices by JAX's collectives and lax.ppermute only.
A program may use at most 64 MiB of HBM per device.

```python
import jax
import jax.numpy as jnp
from jax import lax

RANK = 32
NRHS = 64
LEAF_PTS = 64
NEAR = 8
FAR = 4
DEPTH = 6
LEAF_DEV = 64
LEAVES = 8192
POINTS = 524288
LOCAL_ROWS = 126
LOCAL_ALL = 16128
UPPER_ROWS = 254
N_PTS = 128


def pick_partners(key, targets, usable_mask, first_pick, second_pick, live_count, slots):
    row_count = targets.shape[0]
    col_count = targets.shape[1]
    if col_count < slots:
        pad_count = slots - col_count
        targets = jnp.concatenate([targets, jnp.zeros((row_count, pad_count), jnp.int32)], axis=1)
        usable_mask = jnp.concatenate([usable_mask, jnp.zeros((row_count, pad_count), bool)], axis=1)
        first_pick = jnp.concatenate([first_pick, jnp.zeros((row_count, pad_count), bool)], axis=1)
        second_pick = jnp.concatenate([second_pick, jnp.zeros((row_count, pad_count), bool)], axis=1)
        col_count = slots
    column_ids = jnp.arange(col_count, dtype=jnp.int32)[None, :]
    scores = jax.random.randint(key, (row_count, col_count), 0, 1 << 20, dtype=jnp.int32) * col_count + column_ids
    scores = jnp.where(second_pick, -1, scores)
    scores = jnp.where(first_pick, -2, scores)
    scores = jnp.where(usable_mask, scores, (1 << 29) + column_ids)
    ordering = jnp.argsort(scores, axis=1, stable=True)[:, :slots]
    chosen = jnp.take_along_axis(targets, ordering, axis=1)
    usable = jnp.take_along_axis(usable_mask, ordering, axis=1)
    retained = usable & (jnp.arange(slots, dtype=jnp.int32)[None, :] < live_count[:, None])
    return jnp.where(retained, chosen, -1).astype(jnp.int32)


def draw_near_list(key, part):
    reach_size = LEAF_DEV // 2
    leaf_ids = jnp.arange(LEAVES, dtype=jnp.int32)[:, None]
    shifts = jnp.concatenate([jnp.arange(-reach_size, 0), jnp.arange(1, reach_size + 1)]).astype(jnp.int32)[None, :]
    targets = leaf_ids + shifts
    usable_mask = (targets >= 0) & (targets < LEAVES)
    middle = leaf_ids == LEAVES // 2
    first_pick = middle & (shifts == reach_size)
    second_pick = middle & (shifts == -reach_size)
    key_pick, key_live = jax.random.split(jax.random.fold_in(key, 11))
    flat_ids = jnp.arange(LEAVES, dtype=jnp.int32)
    live_count = jax.random.randint(key_live, (LEAVES,), 1, NEAR, dtype=jnp.int32)
    live_count = jnp.where(flat_ids == LEAVES // 2, NEAR - 1, live_count)
    live_count = jnp.where(flat_ids == 0, 1, live_count)
    others = pick_partners(key_pick, targets, usable_mask, first_pick, second_pick, live_count, NEAR - 1)
    return jnp.concatenate([leaf_ids, others], axis=1).astype(jnp.int32)


def draw_local_partners(key, part):
    pieces = []
    for height in range(DEPTH):
        clusters = LEAF_DEV >> height
        total_count = clusters * N_PTS
        cluster_ids = jnp.arange(total_count, dtype=jnp.int32)[:, None]
        shifts = jnp.concatenate([jnp.arange(-clusters, 0), jnp.arange(1, clusters + 1)]).astype(jnp.int32)[None, :]
        targets = cluster_ids + shifts
        usable_mask = (targets >= 0) & (targets < total_count)
        middle = cluster_ids == total_count // 2
        first_pick = middle & (shifts == clusters)
        second_pick = middle & (shifts == -clusters)
        if height == 0:
            first_pick = first_pick | (cluster_ids == total_count - 2) & (shifts == 1)
        key_pick, key_live = jax.random.split(jax.random.fold_in(key, 100 + height))
        flat_ids = jnp.arange(total_count, dtype=jnp.int32)
        live_count = jax.random.randint(key_live, (total_count,), 1, FAR + 1, dtype=jnp.int32)
        live_count = jnp.where(flat_ids == total_count // 2, FAR, live_count)
        live_count = jnp.where(flat_ids == 0, 1, live_count)
        partner_lists = pick_partners(key_pick, targets, usable_mask, first_pick, second_pick, live_count, FAR)
        pieces.append(partner_lists.reshape(N_PTS, clusters, FAR))
    return jnp.concatenate(pieces, axis=1).reshape(-1, FAR).astype(jnp.int32)


def draw_upper_partners(key, part):
    pieces = []
    top_levels = N_PTS.bit_length() - 1
    for height in range(top_levels):
        clusters = N_PTS >> height
        cluster_ids = jnp.arange(clusters, dtype=jnp.int32)[:, None]
        candidates = jnp.arange(clusters, dtype=jnp.int32)[None, :]
        targets = jnp.broadcast_to(candidates, (clusters, clusters))
        usable_mask = candidates != cluster_ids
        first_pick = (cluster_ids == 0) & (candidates == clusters - 1) & (height == 0)
        second_pick = jnp.zeros((clusters, clusters), bool)
        key_pick, key_live = jax.random.split(jax.random.fold_in(key, 200 + height))
        flat_ids = jnp.arange(clusters, dtype=jnp.int32)
        live_count = jax.random.randint(key_live, (clusters,), 1, FAR + 1, dtype=jnp.int32)
        if height == 0:
            live_count = jnp.where(flat_ids == 0, FAR, live_count)
        pieces.append(pick_partners(key_pick, targets, usable_mask, first_pick, second_pick, live_count, FAR))
    return jnp.concatenate(pieces, axis=0).astype(jnp.int32)


def steps_of(rng, extent, shards, least, top_value):
    gain, own = 1.0, jax.random.fold_in(rng, 6)
    for dim, parts in shards:
        steps = jnp.exp(jax.random.uniform(jax.random.fold_in(own, dim), (parts,), jnp.float32, least / len(shards), top_value / len(shards)))
        gain = gain * jnp.repeat(steps, extent[dim] // parts).reshape([-1 if axis == dim else 1 for axis in range(len(extent))])
    return gain


def centred(stream_key, extent, scale, most, cuts=(), held_as=jnp.bfloat16):
    drawn = scale * jax.random.normal(stream_key, extent, jnp.float32)
    if cuts:
        drawn = drawn * steps_of(stream_key, extent, cuts, -0.22, 0.18)
    return jnp.clip(drawn, -most, most).astype(held_as)


def setup_inputs(seed: int = 0) -> dict:
    key_list = jax.random.split(jax.random.key(seed), 11)
    points = centred(key_list[0], (3, POINTS), 0.8, 4.0, ((1, 128),))
    values = centred(key_list[1], (NRHS, POINTS), 1.0, 6.0, ((0, 4), (1, 128)))
    leaf_basis = centred(key_list[2], (RANK, POINTS), LEAF_PTS ** -0.5, 0.75, ((1, 128),))
    local_transfer = centred(key_list[3], (LOCAL_ALL, RANK, RANK), (2 * RANK) ** -0.5, 0.75, ((0, 128),))
    upper_transfer = centred(key_list[4], (UPPER_ROWS, RANK, RANK), (2 * RANK) ** -0.5, 0.75)
    local_coupling = centred(key_list[5], (LOCAL_ALL, FAR, RANK, RANK), (FAR * RANK) ** -0.5, 0.5, ((0, 128),))
    upper_coupling = centred(key_list[6], (UPPER_ROWS, FAR, RANK, RANK), (FAR * RANK) ** -0.5, 0.5)
    near_list = draw_near_list(jax.random.fold_in(key_list[10], 71), 0)
    local_partners = draw_local_partners(jax.random.fold_in(key_list[10], 71), 0)
    upper_partners = draw_upper_partners(jax.random.fold_in(key_list[10], 71), 0)
    return {"points": points, "values": values, "leaf_basis": leaf_basis, "local_transfer": local_transfer, "upper_transfer": upper_transfer, "local_coupling": local_coupling, "upper_coupling": upper_coupling, "near_list": near_list, "local_partners": local_partners, "upper_partners": upper_partners}


kernel_rate = 1.0


def near_block_terms(targets, slot_rows, present, coords, value_blocks):
    source = jnp.take(coords, slot_rows, axis=1)
    spacing = targets[0][:, None, :, None] - source[0][:, :, None, :]
    distance = spacing * spacing
    spacing = targets[1][:, None, :, None] - source[1][:, :, None, :]
    distance = distance + spacing * spacing
    spacing = targets[2][:, None, :, None] - source[2][:, :, None, :]
    distance = distance + spacing * spacing
    kernel = jnp.where(present[:, :, None, None], jnp.exp(-kernel_rate * distance), jnp.float32(0.0)).astype(jnp.bfloat16)
    fetched = jnp.take(value_blocks, slot_rows, axis=1)
    return jnp.einsum("tjab,ctjb->cta", kernel.astype(jnp.float32), fetched.astype(jnp.float32))


def ascend(matrices, lower):
    terms = jnp.einsum("nrs,nsc->nrc", matrices.astype(jnp.float32), lower.astype(jnp.float32))
    return terms.reshape(terms.shape[0] // 2, 2, terms.shape[1], terms.shape[2]).sum(axis=1).astype(jnp.bfloat16)


def couple_blocks(blocks, source, slot_rows, linked):
    picked = jnp.take(source, slot_rows, axis=0).astype(jnp.float32)
    picked = jnp.where(linked[:, :, None, None], picked, jnp.float32(0.0))
    return jnp.einsum("nfrs,nfsc->nrc", blocks.astype(jnp.float32), picked)


def descend(matrices, coupled, upper):
    spread = jnp.repeat(upper, 2, axis=0).astype(jnp.float32)
    return (coupled + jnp.einsum("nqr,nqc->nrc", matrices.astype(jnp.float32), spread)).astype(jnp.bfloat16)


def reference(points, values, leaf_basis, local_transfer, upper_transfer, local_coupling, upper_coupling, near_list, local_partners, upper_partners):
    coords = points.astype(jnp.float32).reshape(3, LEAVES, LEAF_PTS)
    value_blocks = values.reshape(NRHS, LEAVES, LEAF_PTS)

    def near_group(item):
        first_leaf, partner_rows = item
        targets = lax.dynamic_slice_in_dim(coords, first_leaf, LEAF_DEV, 1)
        present = partner_rows >= 0
        slot_rows = jnp.where(present, partner_rows, 0).astype(jnp.int32)
        return near_block_terms(targets, slot_rows, present, coords, value_blocks)

    starts = (jnp.arange(N_PTS) * LEAF_DEV).astype(jnp.int32)
    grouped = lax.map(near_group, (starts, near_list.reshape(N_PTS, LEAF_DEV, NEAR)))
    near_field = jnp.transpose(grouped, (1, 0, 2, 3)).reshape(NRHS, LEAVES, LEAF_PTS)

    transfers = []
    couplings = []
    partners = []
    for height in range(DEPTH):
        clusters = LEAF_DEV >> height
        offset = 2 * LEAF_DEV - 2 * clusters
        transfers.append(local_transfer.reshape(N_PTS, LOCAL_ROWS, RANK, RANK)[:, offset:offset + clusters].reshape(-1, RANK, RANK))
        couplings.append(local_coupling.reshape(N_PTS, LOCAL_ROWS, FAR, RANK, RANK)[:, offset:offset + clusters].reshape(-1, FAR, RANK, RANK))
        partners.append(local_partners.reshape(N_PTS, LOCAL_ROWS, FAR)[:, offset:offset + clusters].reshape(-1, FAR))
    top_levels = N_PTS.bit_length() - 1
    for height in range(top_levels):
        clusters = N_PTS >> height
        offset = 2 * N_PTS - 2 * clusters
        transfers.append(upper_transfer[offset:offset + clusters])
        couplings.append(upper_coupling[offset:offset + clusters])
        partners.append(upper_partners[offset:offset + clusters])
    levels = DEPTH + top_levels

    leaf_bases = leaf_basis.reshape(RANK, LEAVES, LEAF_PTS)
    upward = [jnp.einsum("rla,cla->lrc", leaf_bases.astype(jnp.float32), value_blocks.astype(jnp.float32)).astype(jnp.bfloat16)]
    for height in range(levels - 1):
        upward.append(ascend(transfers[height], upward[-1]))
    expansion = jnp.zeros((1, RANK, NRHS), jnp.bfloat16)
    for height in reversed(range(levels)):
        linked = partners[height] >= 0
        slot_rows = jnp.where(linked, partners[height], 0).astype(jnp.int32)
        coupled = couple_blocks(couplings[height], upward[height], slot_rows, linked)
        expansion = descend(transfers[height], coupled, expansion)
    far_field = jnp.einsum("rla,lrc->cla", leaf_bases.astype(jnp.float32), expansion.astype(jnp.float32))
    return (near_field + far_field).astype(jnp.bfloat16).reshape(NRHS, POINTS)
```

```python
import functools

import jax
import jax.numpy as jnp
from jax import lax
from jax.experimental import pallas as pl
from jax.experimental.pallas import tpu as pltpu
from jax.sharding import PartitionSpec as P

BF = jnp.bfloat16
F32 = jnp.float32
COLS = 16
RANK = 32
POINTS = 4096
HALF = POINTS // 2
GROUP = 128

LOCAL_BASE = (0, 16, 24, 28, 30, 31)
UPPER_BASE = (0, 32, 48, 56, 60, 62, 63)


def _dot(a, b, ca, cb):
    return lax.dot_general(a, b, (((ca,), (cb,)), ((), ())), preferred_element_type=F32)


def nn(a, b):
    return _dot(a, b, 1, 0)


def nt(a, b):
    return _dot(a, b, 1, 1)


def iota(shape, dim):
    return lax.broadcasted_iota(jnp.int32, shape, dim)


def ones_where(cond):
    return jnp.where(cond, F32(1), F32(0)).astype(BF)


def pair_mask():
    shape = (128, 256)
    return ones_where(iota(shape, 0) // 32 == iota(shape, 1) // 64)


def spread_mask():
    shape = (128, 512)
    row, col = iota(shape, 0), iota(shape, 1)
    return ones_where((row // 32 == col // 128) & (row % 32 == col % 32))


def tile_rows(x):
    return jnp.concatenate([x, x, x, x], axis=0)


def to_chunks(matrix_ref, chunk_ref, count, chunks):
    keep = ones_where(iota((128, count), 1) % 4 == iota((128, count), 0) // 32)
    pick = ones_where(iota((chunks, count), 1) // 4 == iota((chunks, count), 0))
    for r in range(RANK):
        part = tile_rows(matrix_ref[r]) * keep
        chunk_ref[pl.ds(r, chunks, stride=RANK), :] = nt(pick, part)


def chunk_of(ref, index):
    return ref[index * RANK : (index + 1) * RANK, :].astype(BF)


def up_kernel(
    place_ref, values_ref, points_ref, basis_ref, transfer_ref,
    first_ref, second_ref, aug_ref, root_ref, chunks_ref, scratch_ref,
):
    mask = pair_mask()
    to_chunks(transfer_ref, scratch_ref, 126, 32)
    blocks = [chunk_of(scratch_ref, i) for i in range(32)]
    for i in range(32):
        chunks_ref[i] = blocks[i]
    upward = []
    for g in range(16):
        lanes = slice(g * 256, (g + 1) * 256)
        weights = tile_rows(basis_ref[:, lanes]) * mask
        upward.append(nt(values_ref[:, lanes], weights).astype(BF))
    for base, below in ((16, 0), (24, 16), (28, 24), (30, 28)):
        for j in range((base - below) // 2):
            c = below + 2 * j
            weights = tile_rows(jnp.concatenate([blocks[c], blocks[c + 1]], axis=1)) * mask
            children = jnp.concatenate([upward[c], upward[c + 1]], axis=1)
            upward.append(nt(children, weights).astype(BF))
    upward.append(nt(upward[30], tile_rows(blocks[30]) * mask[:, :128]).astype(BF))
    root = nt(upward[31], tile_rows(blocks[31])).astype(BF).astype(F32)
    shape = (COLS, 128)
    root = jnp.where(iota(shape, 0) // 4 == iota(shape, 1) // 32, root, 0.0)
    root = root[:8] + root[8:]
    root = jnp.concatenate([root[:4] + root[4:]] * 2, axis=0).astype(BF)
    for i in range(64):
        root_ref[i * 8 : (i + 1) * 8, :] = root

    coords = points_ref[...].astype(F32)
    square = coords * coords
    square = square[0:1] + square[1:2] + square[2:3]
    high = square.astype(BF).astype(F32)
    middle = (square - high).astype(BF).astype(F32)
    low = (square - high - middle).astype(BF).astype(F32)
    row = iota((16, POINTS), 0)
    aug = jnp.where(row == 0, coords[0:1], jnp.where(row == 1, coords[1:2], coords[2:3]))
    aug = jnp.where(row < 3, aug, jnp.where(row < 6, 1.0, jnp.where(row == 6, -high, jnp.where(row == 7, -middle, -low))))
    aug = jnp.where(row < 9, aug, 0.0).astype(BF)
    aug_ref[...] = aug

    odd = lax.rem(place_ref[0], 2)
    for ref, start in ((first_ref, (1 - odd) * HALF), (second_ref, odd * HALF)):
        start = pl.multiple_of(start, HALF)
        ref[:, 0:HALF] = values_ref[:, pl.ds(start, HALF)]
        ref[:, HALF : 2 * HALF] = aug_ref[:, pl.ds(start, HALF)]
        for i in range(32):
            ref[:, 2 * HALF + i * 128 : 2 * HALF + (i + 1) * 128] = upward[i]


def operator_kernel(
    place_ref, partners_ref, transfer_ref, coupling_ref, order_ref,
    out_ref, blocks_ref, near_ref, spread_ref, weights_ref,
):
    del order_ref
    place = place_ref[0]
    mask = pair_mask()
    to_chunks(transfer_ref, blocks_ref, 254, 64)
    level = iota((8, 254), 0)
    mine = 256 - (256 >> level) + (place >> level)
    chosen = ones_where((iota((8, 254), 1) == mine) & (level < 7))
    for r in range(RANK):
        part = jnp.concatenate([coupling_ref[f, r] for f in range(4)], axis=0)
        near_ref[pl.ds(r, 8, stride=RANK), :] = nt(chosen, part)
    lane_group = iota((RANK, 128), 1) // 32
    chain = ones_where(iota((RANK, 128), 0) == iota((RANK, 128), 1) % 32)
    direct = []
    for k in range(7):
        direct.append(nn(chain[:, :RANK], chunk_of(near_ref, k)).astype(BF))
        if k < 6:
            own = place >> k
            at = pl.multiple_of((UPPER_BASE[k] + (own >> 2)) * RANK, RANK)
            block = blocks_ref[pl.ds(at, RANK), :]
            block = jnp.where(lane_group == (own & 3), block, 0.0).astype(BF)
            chain = nt(chain, tile_rows(block)).astype(BF)
    spread_ref[...] = nn(jnp.concatenate(direct, axis=0), spread_mask())
    weights_ref[...] = jnp.zeros_like(weights_ref)
    for k in range(7):
        row = 256 - (256 >> k) + (place >> k)
        for f in range(4):
            partner = partners_ref[f, row]
            found = jnp.maximum(partner, 0)
            at = pl.multiple_of((UPPER_BASE[k] + (found >> 2)) * RANK, RANK)
            group = jnp.where(partner < 0, -1, found & 3)
            term = spread_ref[k * RANK : (k + 1) * RANK, f * 128 : (f + 1) * 128]
            old = weights_ref[pl.ds(at, RANK), :]
            weights_ref[pl.ds(at, RANK), :] = old + jnp.where(lane_group == group, term, 0.0)
    held = {63: chunk_of(weights_ref, 63)}
    step = nn(held[63], tile_rows(chunk_of(blocks_ref, 62)) * mask[:, :128])
    held[62] = (weights_ref[62 * RANK : 63 * RANK, :] + step).astype(BF)
    for k in (4, 3, 2, 1, 0):
        for j in range((UPPER_BASE[k + 1] - UPPER_BASE[k]) // 2):
            c = UPPER_BASE[k] + 2 * j
            pair = jnp.concatenate([chunk_of(blocks_ref, c), chunk_of(blocks_ref, c + 1)], axis=1)
            step = nn(held[UPPER_BASE[k + 1] + j], tile_rows(pair) * mask)
            for h in range(2):
                total = weights_ref[(c + h) * RANK : (c + h + 1) * RANK, :]
                held[c + h] = (total + step[:, h * 128 : (h + 1) * 128]).astype(BF)
    for c in range(32):
        out_ref[c] = held[c]


def near_kernel(
    place_ref, list_ref, values_ref, aug_ref, first_ref, second_ref,
    near_ref, low_ref, high_ref, target_ref,
):
    place = place_ref[0]
    odd = lax.rem(place, 2)
    shape = (128, 512)
    row, col = iota(shape, 0), iota(shape, 1)
    part = col // 128
    lane = col % 128
    copy = ones_where((lane // 64 == part % 2) & (row == lane % 64 + 64 * (part // 2)))

    def stage(ref, first_leaf, chunks, value_at, aug_source, aug_at):
        rows = []
        for i in range(chunks):
            rows.append(ref[:, value_at + i * 128 : value_at + (i + 1) * 128])
            rows.append(aug_source[:, aug_at + i * 128 : aug_at + (i + 1) * 128])
        out = nn(jnp.concatenate(rows, axis=0), copy).astype(BF)
        for i in range(chunks):
            for h in range(2):
                block = out[i * 32 : (i + 1) * 32, h * 256 : (h + 1) * 256]
                low_ref[first_leaf + 2 * i + h] = block[:, :128]
                high_ref[first_leaf + 2 * i + h] = block[:, 128:]

    stage(values_ref, 32, 16, 0, aug_ref, 0)
    stage(values_ref, 64, 16, HALF, aug_ref, HALF)
    stage(first_ref, pl.multiple_of((1 - odd) * 96, 32), 16, 0, first_ref, HALF)
    stage(second_ref, pl.multiple_of(odd * 96, 32), 16, 0, second_ref, HALF)
    low_ref[128] = jnp.zeros((32, 128), BF)
    high_ref[128] = jnp.zeros((32, 128), BF)

    row, col = iota((16, 16), 0), iota((16, 16), 1)
    swap = jnp.where(
        (row < 3) & (row == col), 2.0,
        jnp.where((row >= 3) & (col >= 3) & (row < 9) & (col < 9) & ((row + 3 == col) | (row == col + 3)), 1.0, 0.0),
    ).astype(BF)
    for i in range(32):
        lanes = slice(i * 128, (i + 1) * 128)
        target_ref[lanes, :] = _dot(aug_ref[:, lanes], swap, 0, 0).astype(BF)

    base = place * 64 - 32

    def pair(m, carry):
        results = []
        for h in range(2):
            leaf = 2 * m + h
            columns = []
            for f in range(0, 8, 2):
                left, right = list_ref[f, leaf], list_ref[f + 1, leaf]
                left = jnp.where(left < 0, 128, left - base)
                right = jnp.where(right < 0, 128, right - base)
                columns.append(low_ref[left] + high_ref[right])
            stack = jnp.concatenate(columns, axis=1)
            targets = target_ref[pl.ds(pl.multiple_of(leaf * 64, 64), 64), :]
            kernel = jnp.exp(nn(targets, stack[16:])).astype(BF)
            results.append(nt(stack[:16], kernel))
        near_ref[:, pl.ds(pl.multiple_of(m * 128, 128), 128)] = jnp.concatenate(results, axis=1)
        return carry

    lax.fori_loop(0, 32, pair, 0, unroll=2)


def far_kernel(
    place_ref, partners_ref, coupling_ref, chunks_ref, basis_ref, near_ref, own_ref, first_ref, second_ref,
    base_ref, basis_out_ref, blocks_ref, spread_ref, coupled_ref,
):
    place = place_ref[0]
    odd = lax.rem(place, 2)
    same = ones_where(iota((128, 126), 0) == iota((128, 126), 1))
    for r in range(RANK):
        part = jnp.concatenate([coupling_ref[f, r] for f in range(4)], axis=0)
        blocks_ref[pl.ds(r, 128, stride=RANK), :] = nt(same, part)
    spread = spread_mask()
    for ref, first in ((own_ref, 128), (first_ref, (1 - odd) * 256), (second_ref, odd * 256)):
        rows = [ref[:, POINTS + i * 128 : POINTS + (i + 1) * 128] for i in range(32)]
        rows = jnp.concatenate(rows, axis=0)
        out = nn(rows, spread).astype(BF)
        for i in range(32):
            for j in range(4):
                block = out[i * COLS : (i + 1) * COLS, j * 128 : (j + 1) * 128]
                spread_ref[first + 4 * i + j] = block
    spread_ref[384] = jnp.zeros((COLS, 128), BF)

    group = iota((COLS, 128), 1) // 32
    slot_masks = [ones_where(group == f) for f in range(4)]
    zero = jnp.zeros((RANK, 128), BF)
    nothing = jnp.zeros((COLS, 128), BF)

    def couple(chunk, height, live):
        shift = 6 - height
        offset = 128 - (128 >> height)
        lefts, rights = [], []
        for j in range(4):
            if j >= live:
                lefts.append(nothing)
                rights.append(jnp.concatenate([zero] * 4, axis=1))
                continue
            total = nothing
            for f in range(4):
                partner = partners_ref[f, chunk * 4 + j]
                relative = partner - ((place - 1) << shift)
                at = ((relative >> shift) << 7) + offset + (relative & ((1 << shift) - 1))
                at = jnp.where(partner < 0, 384, at)
                total = total + spread_ref[at] * slot_masks[f]
            lefts.append(total)
            block = blocks_ref[pl.ds(pl.multiple_of((chunk * 4 + j) * RANK, RANK), RANK), :].astype(BF)
            rights.append(jnp.concatenate([zero] * j + [block] + [zero] * (3 - j), axis=1))
        result = nt(jnp.concatenate(lefts, axis=1), jnp.concatenate(rights, axis=0))
        coupled_ref[pl.ds(pl.multiple_of(chunk * COLS, COLS), COLS), :] = result

    for height in range(6):
        first = LOCAL_BASE[height]
        count = 16 >> height if height < 5 else 1
        if count >= 4:
            lax.fori_loop(0, count, lambda i, c, f=first, h=height: (couple(f + i, h, 4), c)[1], 0, unroll=2)
        else:
            for i in range(count):
                couple(first + i, height, 4 if height < 5 else 2)

    mask = pair_mask()
    pad = jnp.zeros((RANK, 128), F32)

    def coupled(c):
        return coupled_ref[c * COLS : (c + 1) * COLS, :]

    held = {31: jnp.concatenate([coupled(31).astype(BF), chunks_ref[31]], axis=0)}
    step = nn(held[31], tile_rows(chunks_ref[30]) * mask[:, :128])
    held[30] = (step + jnp.concatenate([coupled(30), pad], axis=0)).astype(BF)
    for height in (3, 2, 1, 0):
        for j in range((LOCAL_BASE[height + 1] - LOCAL_BASE[height]) // 2):
            c = LOCAL_BASE[height] + 2 * j
            pair = jnp.concatenate([chunks_ref[c], chunks_ref[c + 1]], axis=1)
            step = nn(held[LOCAL_BASE[height + 1] + j], tile_rows(pair) * mask)
            for h in range(2):
                extra = jnp.concatenate([coupled(c + h), pad], axis=0)
                held[c + h] = (step[:, h * 128 : (h + 1) * 128] + extra).astype(BF)
    for g in range(16):
        lanes = slice(g * 256, (g + 1) * 256)
        out = nn(held[g], tile_rows(basis_ref[:, lanes]) * mask)
        base_ref[:, lanes] = near_ref[:, lanes] + out[:COLS]
        basis_out_ref[:, lanes] = out[COLS:].astype(BF)


def final_kernel(roots_ref, operator_ref, basis_ref, base_ref, out_ref):
    roots = roots_ref[...].astype(F32)
    roots = roots.reshape(32, COLS, 128)
    shape = (32, COLS, 128)
    device, column = iota(shape, 2) // 32, iota(shape, 1) // 4
    total = jnp.where(device == column, roots, 0.0)
    for d in range(1, 4):
        moved = pltpu.roll(pltpu.roll(roots, COLS - 4 * d, 1), 32 * d, 2)
        total = jnp.where(device == (column + d) % 4, moved, total)
    total = total.astype(BF)
    left = jnp.concatenate([total[i] for i in range(32)], axis=1)
    right = jnp.concatenate([operator_ref[i] for i in range(32)], axis=1)
    expansion = nt(left, right).astype(BF)
    for g in range(8):
        lanes = slice(g * 512, (g + 1) * 512)
        out_ref[:, lanes] = (base_ref[:, lanes] + nn(expansion, basis_ref[:, lanes])).astype(BF)


SMEM = pl.BlockSpec(memory_space=pltpu.SMEM)
VMEM = pl.BlockSpec(memory_space=pltpu.VMEM)
ANY = pl.BlockSpec(memory_space=pl.ANY)
SCRATCH = pltpu.VMEM


def call(kernel, ins, outs, scratch, name, interpret=False):
    return pl.pallas_call(
        kernel,
        in_specs=ins,
        out_specs=[VMEM] * len(outs),
        out_shape=[jax.ShapeDtypeStruct(s, d) for s, d in outs],
        scratch_shapes=scratch,
        compiler_params=pltpu.CompilerParams(vmem_limit_bytes=48 * 1024 * 1024),
        name=name,
        interpret=interpret,
    )


def kernels(interpret=False):
    up = call(
        up_kernel,
        [SMEM, VMEM, VMEM, VMEM, VMEM],
        [
            ((COLS, 2 * POINTS), BF),
            ((COLS, 2 * POINTS), BF),
            ((16, POINTS), BF),
            ((4 * GROUP, 128), BF),
            ((32, RANK, 128), BF),
        ],
        [SCRATCH((32 * RANK, 128), F32)],
        "up",
        interpret,
    )
    operator = call(
        operator_kernel,
        [SMEM, SMEM, VMEM, VMEM, ANY],
        [((32, RANK, 128), BF)],
        [
            SCRATCH((64 * RANK, 128), F32),
            SCRATCH((8 * RANK, 128), F32),
            SCRATCH((7 * RANK, 512), F32),
            SCRATCH((64 * RANK, 128), F32),
        ],
        "operator",
        interpret,
    )
    near = call(
        near_kernel,
        [SMEM, SMEM, VMEM, VMEM, VMEM, VMEM],
        [((COLS, POINTS), F32)],
        [SCRATCH((129, 32, 128), BF), SCRATCH((129, 32, 128), BF), SCRATCH((POINTS, 16), BF)],
        "near",
        interpret,
    )
    far = call(
        far_kernel,
        [SMEM, SMEM, VMEM, VMEM, VMEM, VMEM, VMEM, VMEM, VMEM],
        [((COLS, POINTS), F32), ((RANK, POINTS), BF)],
        [SCRATCH((128 * RANK, 128), F32), SCRATCH((385, COLS, 128), BF), SCRATCH((32 * COLS, 128), F32)],
        "far",
        interpret,
    )
    final = call(final_kernel, [VMEM] * 4, [((COLS, POINTS), BF)], [], "final", interpret)
    return up, operator, near, far, final


def shards(
    points, values, leaf_basis, local_transfer, upper_transfer, local_coupling, upper_coupling,
    near_list, local_partners, upper_partners,
):
    up, operator, near, far, final = kernels()
    place = lax.axis_index("pts").astype(jnp.int32).reshape(1)
    local_t = jnp.transpose(local_transfer, (1, 2, 0))
    upper_t = jnp.transpose(upper_transfer, (1, 2, 0))
    local_c = jnp.transpose(local_coupling, (1, 2, 3, 0))
    upper_c = jnp.transpose(upper_coupling, (1, 2, 3, 0))
    first, second, aug, root, chunks = up(place, values, points, leaf_basis, local_t)
    roots = lax.all_to_all(root.reshape(GROUP, 4, 128), "pts", 0, 0, tiled=True)
    inside = [(i, i ^ 1) for i in range(GROUP)]
    across = [(i, ((i + 1) ^ 1) - 1) for i in range(1, GROUP - 1)]
    first_in = lax.ppermute(first, "pts", inside)
    second_in = lax.ppermute(second, "pts", across)
    (op,) = operator(place, upper_partners.T, upper_t, upper_c, chunks)
    (near_field,) = near(place, near_list.T, values, aug, first_in, second_in)
    base, basis = far(place, local_partners.T, local_c, chunks, leaf_basis, near_field, first, first_in, second_in)
    (out,) = final(roots.reshape(4 * GROUP, 128), op, basis, base)
    return out


def solution(mesh):
    placed = (
        P(None, "pts"),
        P("rhs", "pts"),
        P(None, "pts"),
        P("pts", None, None),
        P(),
        P("pts", None, None, None),
        P(),
        P("pts", None),
        P("pts", None),
        P(),
    )
    return jax.shard_map(
        shards, mesh=mesh, in_specs=placed, out_specs=P("rhs", "pts"), check_vma=False
    )
```

```python
import functools

import jax
import jax.numpy as jnp
from jax import lax
from jax.experimental import pallas as pl
from jax.experimental.pallas import tpu as pltpu
from jax.sharding import PartitionSpec as P

BF = jnp.bfloat16
F32 = jnp.float32
COLS = 16
RANK = 32
POINTS = 4096
HALF = POINTS // 2
GROUP = 128

PITCH = RANK + 1
LEAVES_PER_STEP = 8

LOCAL_BASE = (0, 16, 24, 28, 30, 31)
UPPER_BASE = (0, 32, 48, 56, 60, 62, 63)


def _dot(a, b, ca, cb):
    return lax.dot_general(a, b, (((ca,), (cb,)), ((), ())), preferred_element_type=F32)


def nn(a, b):
    return _dot(a, b, 1, 0)


def nt(a, b):
    return _dot(a, b, 1, 1)


def iota(shape, dim):
    return lax.broadcasted_iota(jnp.int32, shape, dim)


def ones_where(cond):
    return jnp.where(cond, F32(1), F32(0)).astype(BF)


def pair_mask():
    shape = (128, 256)
    return ones_where(iota(shape, 0) // 32 == iota(shape, 1) // 64)


def spread_mask():
    shape = (128, 512)
    row, col = iota(shape, 0), iota(shape, 1)
    return ones_where((row // 32 == col // 128) & (row % 32 == col % 32))


def tile_rows(x):
    return jnp.concatenate([x, x, x, x], axis=0)


def to_chunks(matrix_ref, chunk_ref, count, chunks):
    keep = ones_where(iota((128, count), 1) % 4 == iota((128, count), 0) // 32)
    pick = ones_where(iota((chunks, count), 1) // 4 == iota((chunks, count), 0))
    for r in range(RANK):
        part = tile_rows(matrix_ref[r]) * keep
        chunk_ref[pl.ds(r, chunks, stride=PITCH), :] = nt(pick, part)


def chunk_of(ref, index):
    return ref[index * PITCH : index * PITCH + RANK, :].astype(BF)


def fetch_all(pairs, sems):
    copies = [pltpu.make_async_copy(a, b, sems.at[i]) for i, (a, b) in enumerate(pairs)]
    for copy in copies:
        copy.start()
    return copies


def up_kernel(
    place_ref, values_in, points_in, basis_in, transfer_in,
    first_ref, second_ref, aug_ref, root_ref, chunks_ref,
    values_ref, basis_ref, points_ref, transfer_ref, scratch_ref, sems,
):
    pairs = (
        (transfer_in, transfer_ref), (values_in, values_ref), (basis_in, basis_ref), (points_in, points_ref),
    )
    copies = fetch_all(pairs, sems)
    mask = pair_mask()
    copies[0].wait()
    to_chunks(transfer_ref, scratch_ref, 126, 32)
    blocks = [chunk_of(scratch_ref, i) for i in range(32)]
    for i in range(32):
        chunks_ref[i] = blocks[i]
    copies[1].wait()
    copies[2].wait()
    upward = []
    for g in range(16):
        lanes = slice(g * 256, (g + 1) * 256)
        weights = tile_rows(basis_ref[:, lanes]) * mask
        upward.append(nt(values_ref[:, lanes], weights).astype(BF))
    for base, below in ((16, 0), (24, 16), (28, 24), (30, 28)):
        for j in range((base - below) // 2):
            c = below + 2 * j
            weights = tile_rows(jnp.concatenate([blocks[c], blocks[c + 1]], axis=1)) * mask
            children = jnp.concatenate([upward[c], upward[c + 1]], axis=1)
            upward.append(nt(children, weights).astype(BF))
    upward.append(nt(upward[30], tile_rows(blocks[30]) * mask[:, :128]).astype(BF))
    root = nt(upward[31], tile_rows(blocks[31])).astype(BF).astype(F32)
    shape = (COLS, 128)
    root = jnp.where(iota(shape, 0) // 4 == iota(shape, 1) // 32, root, 0.0)
    root = root[:8] + root[8:]
    root = jnp.concatenate([root[:4] + root[4:]] * 2, axis=0).astype(BF)
    for i in range(64):
        root_ref[i * 8 : (i + 1) * 8, :] = root

    copies[3].wait()
    for g in range(8):
        lanes = slice(g * 512, (g + 1) * 512)
        coords = points_ref[:, lanes].astype(F32)
        square = coords * coords
        square = square[0:1] + square[1:2] + square[2:3]
        high = square.astype(BF).astype(F32)
        middle = (square - high).astype(BF).astype(F32)
        low = (square - high - middle).astype(BF).astype(F32)
        row = iota((8, 512), 0)
        top = jnp.where(row == 0, coords[0:1], jnp.where(row == 1, coords[1:2], coords[2:3]))
        top = jnp.where(row < 3, top, jnp.where(row < 6, 1.0, jnp.where(row == 6, -high, -middle)))
        bottom = jnp.where(row == 0, -low, 0.0)
        aug_ref[:, lanes] = jnp.concatenate([top, bottom], axis=0).astype(BF)

    odd = lax.rem(place_ref[0], 2)
    for ref, start in ((first_ref, (1 - odd) * HALF), (second_ref, odd * HALF)):
        start = pl.multiple_of(start, HALF)
        ref[:, 0:HALF] = values_ref[:, pl.ds(start, HALF)]
        ref[:, HALF : 2 * HALF] = aug_ref[:, pl.ds(start, HALF)]
        for i in range(32):
            ref[:, 2 * HALF + i * 128 : 2 * HALF + (i + 1) * 128] = upward[i]


def operator_part(
    place, partners_ref, transfer_ref, coupling_ref, out_ref, blocks_ref, near_ref, spread_ref, weights_ref, waits,
):
    mask = pair_mask()
    waits[0].wait()
    to_chunks(transfer_ref, blocks_ref, 254, 64)
    level = iota((8, 254), 0)
    mine = 256 - (256 >> level) + (place >> level)
    chosen = ones_where((iota((8, 254), 1) == mine) & (level < 7))
    waits[1].wait()
    for r in range(RANK):
        part = jnp.concatenate([coupling_ref[f, r] for f in range(4)], axis=0)
        near_ref[pl.ds(r, 8, stride=PITCH), :] = nt(chosen, part)
    lane_group = iota((RANK, 128), 1) // 32
    chain = ones_where(iota((RANK, 128), 0) == iota((RANK, 128), 1) % 32)
    direct = []
    for k in range(7):
        direct.append(nn(chain[:, :RANK], chunk_of(near_ref, k)).astype(BF))
        if k < 6:
            own = place >> k
            block = blocks_ref[pl.ds((UPPER_BASE[k] + (own >> 2)) * PITCH, RANK), :]
            block = jnp.where(lane_group == (own & 3), block, 0.0).astype(BF)
            chain = nt(chain, tile_rows(block)).astype(BF)
    spread_ref[...] = nn(jnp.concatenate(direct, axis=0), spread_mask())
    weights_ref[...] = jnp.zeros_like(weights_ref)
    waits[2].wait()
    for k in range(7):
        row = 256 - (256 >> k) + (place >> k)
        for f in range(4):
            partner = partners_ref[f, row]
            found = jnp.maximum(partner, 0)
            at = pl.multiple_of((UPPER_BASE[k] + (found >> 2)) * RANK, RANK)
            group = jnp.where(partner < 0, -1, found & 3)
            term = spread_ref[k * RANK : (k + 1) * RANK, f * 128 : (f + 1) * 128]
            old = weights_ref[pl.ds(at, RANK), :]
            weights_ref[pl.ds(at, RANK), :] = old + jnp.where(lane_group == group, term, 0.0)
    held = {63: weights_ref[63 * RANK : 64 * RANK, :].astype(BF)}
    step = nn(held[63], tile_rows(chunk_of(blocks_ref, 62)) * mask[:, :128])
    held[62] = (weights_ref[62 * RANK : 63 * RANK, :] + step).astype(BF)
    for k in (4, 3, 2, 1, 0):
        for j in range((UPPER_BASE[k + 1] - UPPER_BASE[k]) // 2):
            c = UPPER_BASE[k] + 2 * j
            pair = jnp.concatenate([chunk_of(blocks_ref, c), chunk_of(blocks_ref, c + 1)], axis=1)
            step = nn(held[UPPER_BASE[k + 1] + j], tile_rows(pair) * mask)
            for h in range(2):
                total = weights_ref[(c + h) * RANK : (c + h + 1) * RANK, :]
                held[c + h] = (total + step[:, h * 128 : (h + 1) * 128]).astype(BF)
    for c in range(32):
        out_ref[c] = held[c]


def near_part(
    place, list_ref, values_ref, aug_ref, first_ref, second_ref, near_ref, low_ref, high_ref, target_ref, waits,
):
    waits[0].wait()
    odd = lax.rem(place, 2)
    lane = iota((32, 128), 1)
    in_low, in_high = ones_where(lane < 64), ones_where(lane >= 64)

    def stage(ref, first_leaf, value_at, aug_source, aug_at):
        for i in range(16):
            block = jnp.concatenate(
                [
                    ref[:, value_at + i * 128 : value_at + (i + 1) * 128],
                    aug_source[:, aug_at + i * 128 : aug_at + (i + 1) * 128],
                ],
                axis=0,
            )
            turned = pltpu.roll(block.astype(F32), 64, 1).astype(BF)
            low_ref[first_leaf + 2 * i] = block * in_low
            high_ref[first_leaf + 2 * i] = turned * in_high
            low_ref[first_leaf + 2 * i + 1] = turned * in_low
            high_ref[first_leaf + 2 * i + 1] = block * in_high

    stage(values_ref, 32, 0, aug_ref, 0)
    stage(values_ref, 64, HALF, aug_ref, HALF)
    stage(first_ref, (1 - odd) * 96, 0, first_ref, HALF)
    stage(second_ref, odd * 96, 0, second_ref, HALF)
    low_ref[128] = jnp.zeros((32, 128), BF)
    high_ref[128] = jnp.zeros((32, 128), BF)

    row, col = iota((16, 16), 0), iota((16, 16), 1)
    swap = jnp.where(
        (row < 3) & (row == col), 2.0,
        jnp.where((row >= 3) & (col >= 3) & (row < 9) & (col < 9) & ((row + 3 == col) | (row == col + 3)), 1.0, 0.0),
    ).astype(BF)
    for i in range(32):
        lanes = slice(i * 128, (i + 1) * 128)
        target_ref[lanes, :] = _dot(aug_ref[:, lanes], swap, 0, 0).astype(BF)

    base = place * 64 - 32
    waits[1].wait()

    def step(m, carry):
        stacks = []
        for h in range(LEAVES_PER_STEP):
            leaf = LEAVES_PER_STEP * m + h
            columns = []
            for f in range(0, 8, 2):
                left, right = list_ref[f, leaf], list_ref[f + 1, leaf]
                left = jnp.where(left < 0, 128, left - base)
                right = jnp.where(right < 0, 128, right - base)
                columns.append(low_ref[left] + high_ref[right])
            stacks.append(jnp.concatenate(columns, axis=1))
        kernel = []
        for h in range(LEAVES_PER_STEP):
            leaf = LEAVES_PER_STEP * m + h
            targets = target_ref[pl.ds(pl.multiple_of(leaf * 64, 64), 64), :]
            kernel.append(jnp.exp(nn(targets, stacks[h][16:])).astype(BF))
        results = [nt(stacks[h][:16], kernel[h]) for h in range(LEAVES_PER_STEP)]
        width = 64 * LEAVES_PER_STEP
        near_ref[:, pl.ds(pl.multiple_of(m * width, width), width)] = jnp.concatenate(results, axis=1)
        return carry

    lax.fori_loop(0, 64 // LEAVES_PER_STEP, step, 0)


def far_part(
    place, partners_ref, coupling_ref, chunks_ref, basis_ref, own_ref, first_ref, second_ref,
    base_ref, basis_out_ref, blocks_ref, spread_ref, coupled_ref, waits,
):
    waits[0].wait()
    odd = lax.rem(place, 2)
    same = ones_where(iota((128, 126), 0) == iota((128, 126), 1))
    for r in range(RANK):
        part = jnp.concatenate([coupling_ref[f, r] for f in range(4)], axis=0)
        blocks_ref[pl.ds(r, 128, stride=PITCH), :] = nt(same, part)
    spread = spread_mask()
    for ref, piece in ((own_ref, 1), (first_ref, (1 - odd) * 2), (second_ref, odd * 2)):
        rows = [ref[:, POINTS + i * 128 : POINTS + (i + 1) * 128] for i in range(32)]
        out = nn(jnp.concatenate(rows, axis=0), spread).astype(BF)
        for height in range(6):
            clusters = 64 >> height
            offset = 128 - 2 * clusters
            first = 3 * offset + piece * clusters
            for j in range(clusters):
                i, group = divmod(offset + j, 4)
                block = out[i * COLS : (i + 1) * COLS, group * 128 : (group + 1) * 128]
                spread_ref[first + j] = block
    spread_ref[384] = jnp.zeros((COLS, 128), BF)
    waits[1].wait()

    group = iota((COLS, 128), 1) // 32
    slot_masks = [ones_where(group == f) for f in range(4)]
    zero = jnp.zeros((RANK, 128), BF)
    nothing = jnp.zeros((COLS, 128), BF)

    def couple(chunk, height, live):
        base = 3 * (128 - (128 >> height)) - ((place - 1) << (6 - height))
        lefts, rights = [], []
        for j in range(4):
            if j >= live:
                lefts.append(nothing)
                rights.append(jnp.concatenate([zero] * 4, axis=1))
                continue
            total = nothing
            for f in range(4):
                partner = partners_ref[f, chunk * 4 + j]
                at = jnp.where(partner < 0, 384, partner + base)
                total = total + spread_ref[at] * slot_masks[f]
            lefts.append(total)
            block = blocks_ref[pl.ds((chunk * 4 + j) * PITCH, RANK), :].astype(BF)
            rights.append(jnp.concatenate([zero] * j + [block] + [zero] * (3 - j), axis=1))
        result = nt(jnp.concatenate(lefts, axis=1), jnp.concatenate(rights, axis=0))
        coupled_ref[pl.ds(pl.multiple_of(chunk * COLS, COLS), COLS), :] = result

    for height in range(6):
        first = LOCAL_BASE[height]
        count = 16 >> height if height < 5 else 1
        if count >= 4:
            lax.fori_loop(0, count, lambda i, c, f=first, h=height: (couple(f + i, h, 4), c)[1], 0, unroll=2)
        else:
            for i in range(count):
                couple(first + i, height, 4 if height < 5 else 2)

    waits[2].wait()
    mask = pair_mask()
    pad = jnp.zeros((RANK, 128), F32)

    def coupled(c):
        return coupled_ref[c * COLS : (c + 1) * COLS, :]

    held = {31: jnp.concatenate([coupled(31).astype(BF), chunks_ref[31]], axis=0)}
    step = nn(held[31], tile_rows(chunks_ref[30]) * mask[:, :128])
    held[30] = (step + jnp.concatenate([coupled(30), pad], axis=0)).astype(BF)
    for height in (3, 2, 1, 0):
        for j in range((LOCAL_BASE[height + 1] - LOCAL_BASE[height]) // 2):
            c = LOCAL_BASE[height] + 2 * j
            pair = jnp.concatenate([chunks_ref[c], chunks_ref[c + 1]], axis=1)
            step = nn(held[LOCAL_BASE[height + 1] + j], tile_rows(pair) * mask)
            for h in range(2):
                extra = jnp.concatenate([coupled(c + h), pad], axis=0)
                held[c + h] = (step[:, h * 128 : (h + 1) * 128] + extra).astype(BF)
    for g in range(16):
        lanes = slice(g * 256, (g + 1) * 256)
        out = nn(held[g], tile_rows(basis_ref[:, lanes]) * mask)
        base_ref[:, lanes] += out[:COLS]
        basis_out_ref[:, lanes] = out[COLS:].astype(BF)


def main_kernel(
    place_ref, upper_partners_in, partners_in, list_in, upper_transfer_in, upper_coupling_in, coupling_in, values_in,
    basis_in, aug_ref, chunks_ref, own_ref, first_ref, second_ref,
    operator_ref, base_ref, basis_out_ref,
    upper_partners_ref, partners_ref, list_ref, upper_transfer_ref, upper_coupling_ref, coupling_ref, values_ref,
    basis_ref, upper_blocks_ref, picked_ref, terms_ref, weights_ref, low_ref, high_ref, target_ref, blocks_ref,
    spread_ref, coupled_ref, sems,
):
    pairs = (
        (upper_transfer_in, upper_transfer_ref), (upper_coupling_in, upper_coupling_ref),
        (upper_partners_in, upper_partners_ref), (values_in, values_ref), (list_in, list_ref),
        (coupling_in, coupling_ref), (partners_in, partners_ref), (basis_in, basis_ref),
    )
    copies = fetch_all(pairs, sems)
    place = place_ref[0]
    operator_part(
        place, upper_partners_ref, upper_transfer_ref, upper_coupling_ref, operator_ref, upper_blocks_ref,
        picked_ref, terms_ref, weights_ref, copies[0:3],
    )
    near_part(
        place, list_ref, values_ref, aug_ref, first_ref, second_ref, base_ref, low_ref, high_ref, target_ref,
        copies[3:5],
    )
    far_part(
        place, partners_ref, coupling_ref, chunks_ref, basis_ref, own_ref, first_ref, second_ref, base_ref,
        basis_out_ref, blocks_ref, spread_ref, coupled_ref, copies[5:8],
    )


def final_kernel(roots_ref, operator_ref, basis_ref, base_ref, out_ref):
    roots = roots_ref[...].astype(F32)
    roots = roots.reshape(32, COLS, 128)
    shape = (32, COLS, 128)
    device, column = iota(shape, 2) // 32, iota(shape, 1) // 4
    total = jnp.where(device == column, roots, 0.0)
    for d in range(1, 4):
        moved = pltpu.roll(pltpu.roll(roots, COLS - 4 * d, 1), 32 * d, 2)
        total = jnp.where(device == (column + d) % 4, moved, total)
    total = total.astype(BF)
    left = jnp.concatenate([total[i] for i in range(32)], axis=1)
    right = jnp.concatenate([operator_ref[i] for i in range(32)], axis=1)
    expansion = nt(left, right).astype(BF)
    for g in range(8):
        lanes = slice(g * 512, (g + 1) * 512)
        out_ref[:, lanes] = (base_ref[:, lanes] + nn(expansion, basis_ref[:, lanes])).astype(BF)


SMEM = pl.BlockSpec(memory_space=pltpu.SMEM)
VMEM = pl.BlockSpec(memory_space=pltpu.VMEM)
HBM = pl.BlockSpec(memory_space=pltpu.HBM)
SCRATCH = pltpu.VMEM
DMA = pltpu.SemaphoreType.DMA


def call(kernel, ins, outs, scratch, name, interpret=False):
    return pl.pallas_call(
        kernel,
        in_specs=ins,
        out_specs=[VMEM] * len(outs),
        out_shape=[jax.ShapeDtypeStruct(s, d) for s, d in outs],
        scratch_shapes=scratch,
        compiler_params=pltpu.CompilerParams(vmem_limit_bytes=32 * 1024 * 1024),
        name=name,
        interpret=interpret,
    )


def kernels(interpret=False):
    up = call(
        up_kernel,
        [SMEM] + [HBM] * 4,
        [
            ((COLS, 2 * POINTS), BF),
            ((COLS, 2 * POINTS), BF),
            ((16, POINTS), BF),
            ((4 * GROUP, 128), BF),
            ((32, RANK, 128), BF),
        ],
        [
            SCRATCH((COLS, POINTS), BF),
            SCRATCH((RANK, POINTS), BF),
            SCRATCH((3, POINTS), BF),
            SCRATCH((RANK, RANK, 126), BF),
            SCRATCH((32 * PITCH, 128), F32),
            DMA((4,)),
        ],
        "up",
        interpret,
    )
    main = call(
        main_kernel,
        [SMEM] + [HBM] * 8 + [VMEM] * 5,
        [((32, RANK, 128), BF), ((COLS, POINTS), F32), ((RANK, POINTS), BF)],
        [
            pltpu.SMEM((4, 254), jnp.int32),
            pltpu.SMEM((4, 126), jnp.int32),
            pltpu.SMEM((8, 64), jnp.int32),
            SCRATCH((RANK, RANK, 254), BF),
            SCRATCH((4, RANK, RANK, 254), BF),
            SCRATCH((4, RANK, RANK, 126), BF),
            SCRATCH((COLS, POINTS), BF),
            SCRATCH((RANK, POINTS), BF),
            SCRATCH((64 * PITCH, 128), F32),
            SCRATCH((8 * PITCH, 128), F32),
            SCRATCH((7 * RANK, 512), F32),
            SCRATCH((64 * RANK, 128), F32),
            SCRATCH((129, 32, 128), BF),
            SCRATCH((129, 32, 128), BF),
            SCRATCH((POINTS, 16), BF),
            SCRATCH((128 * PITCH, 128), F32),
            SCRATCH((385, COLS, 128), BF),
            SCRATCH((32 * COLS, 128), F32),
            DMA((8,)),
        ],
        "main",
        interpret,
    )
    final = call(final_kernel, [VMEM] * 4, [((COLS, POINTS), BF)], [], "final", interpret)
    return up, main, final


def shards(
    points, values, leaf_basis, local_transfer, upper_transfer, local_coupling, upper_coupling,
    near_list, local_partners, upper_partners,
):
    up, main, final = kernels()
    place = lax.axis_index("pts").astype(jnp.int32).reshape(1)
    local_t = jnp.transpose(local_transfer, (1, 2, 0))
    upper_t = jnp.transpose(upper_transfer, (1, 2, 0))
    local_c = jnp.transpose(local_coupling, (1, 2, 3, 0))
    upper_c = jnp.transpose(upper_coupling, (1, 2, 3, 0))
    values, points, leaf_basis, local_t, upper_t, upper_c, local_c, near_list, local_partners, upper_partners = (
        pltpu.with_memory_space_constraint(x, pltpu.HBM)
        for x in (
            values, points, leaf_basis, local_t, upper_t, upper_c, local_c, near_list.T, local_partners.T, upper_partners.T
        )
    )
    first, second, aug, root, chunks = up(place, values, points, leaf_basis, local_t)
    roots = lax.all_to_all(root.reshape(GROUP, 4, 128), "pts", 0, 0, tiled=True)
    inside = [(i, i ^ 1) for i in range(GROUP)]
    across = [(i, ((i + 1) ^ 1) - 1) for i in range(1, GROUP - 1)]
    first_in = lax.ppermute(first, "pts", inside)
    second_in = lax.ppermute(second, "pts", across)
    op, base, basis = main(
        place, upper_partners, local_partners, near_list, upper_t, upper_c, local_c, values, leaf_basis,
        aug, chunks, first, first_in, second_in,
    )
    (out,) = final(roots.reshape(4 * GROUP, 128), op, basis, base)
    return out


def solution(mesh):
    placed = (
        P(None, "pts"),
        P("rhs", "pts"),
        P(None, "pts"),
        P("pts", None, None),
        P(),
        P("pts", None, None, None),
        P(),
        P("pts", None),
        P("pts", None),
        P(),
    )
    return jax.shard_map(
        shards, mesh=mesh, in_specs=placed, out_specs=P("rhs", "pts"), check_vma=False
    )
```
